32 devices in a mesh: sector: 4 (over y, x), box: 8 (over z, core).
Axes of the slice: x: 2, y: 2, z: 4, core: 2. Of those that a mesh axis runs over, the one named last changes fastest.
Arguments:
- positions: float32 [3, 4, 512, 128], P(None, 'sector', 'box'), may hold values from -0.9 to 0.9
- strengths: float32 [3, 4, 512, 128], P(None, 'sector', 'box'), may hold values from -6 to 6
- counts: int32 [4, 512], P('sector', 'box'), may hold values from 1 to 128
- cross_slot: int32 [4, 2048], P('sector', 'box'), may hold values from 0 to 8191, as said below
- arrive_box: int32 [4, 2048], P('sector', 'box'), may hold values from 0 to 63
- il_source: int32 [4, 512, 16], P('sector', 'box'), may hold values from 0 to 63
- il_class: int32 [4, 512, 16], P('sector', 'box'), may hold values from 0 to 3
- m2m: bfloat16 [4, 441, 441], replicated, may hold values from -0.125 to 0.125
- m2l_leaf: bfloat16 [4, 441, 441], replicated, may hold values from -0.0625 to 0.0625
- tree_up: bfloat16 [2, 441, 441], replicated, may hold values from -0.21875 to 0.21875
- tree_m2l: bfloat16 [2, 441, 441], replicated, may hold values from -0.25 to 0.25
- m2l_sector: bfloat16 [3, 441, 441], replicated, may hold values from -0.15625 to 0.15625
Outputs:
- new_positions: float32 [3, 4, 512, 128], P(None, 'sector', 'box')
- velocity: float32 [3, 4, 512, 128], P(None, 'sector', 'box')
The draws below stay inside these ranges and needn't reach their ends.
Inputs may be any that keep to these rules, and one draw needn't show every extreme that they name: `cross_slot`: within one block's 256 entries the slot numbers are distinct; a slot beyond its box's count carries nothing.
All inputs are finite; a program needn't handle non-finite values.
Results may differ from the reference program's by a relative error of at most 0.006.
Values may be sent and summed in bfloat16 or wider, within the bound.
No kernel may reach another device: no remote copies, remote signals or barrier semaphores. Data moves between devices by JAX's collectives and lax.ppermute only.
A program may use at most 128 MiB of HBM per device.

```python
import math
import jax
import jax.numpy as jnp
from jax import lax

TERMS = 21
COEF = 441
SLOTS = 128
LEVELS_DEV = 3
BOX_DEV = 64
CROSS_DEV = 256
IL = 16
NCLASS = 4
SECTORS = 4
BOXES = 512
N_BOX = 8


def choose_slots(subkey):
    return jax.random.permutation(subkey, BOX_DEV * SLOTS)[:CROSS_DEV]


def draw_cross_slot(key, part):
    block_count = SECTORS * (BOXES // BOX_DEV)
    key_list = jax.random.split(key, block_count)
    chosen = jax.vmap(choose_slots)(key_list)
    return chosen.reshape(SECTORS, BOXES // BOX_DEV * CROSS_DEV).astype(jnp.int32)


def set_ends(values, rng, least, top_value):
    spot = [jax.random.randint(jax.random.fold_in(rng, axis), (), 0, length) for axis, length in enumerate(values.shape)]
    main_axis = values.shape.index(max(values.shape))
    neighbour = spot[:main_axis] + [(spot[main_axis] + 1) % values.shape[main_axis]] + spot[main_axis + 1:]
    return values.at[tuple(spot)].set(least).at[tuple(neighbour)].set(top_value)


def block_levels(own_key, extent, shards, low, top_value):
    def one(axis_at, blocks):
        steps = jax.random.uniform(jax.random.fold_in(jax.random.fold_in(own_key, 6), axis_at), (blocks,), jnp.float32, low / len(shards), top_value / len(shards))
        return jnp.repeat(jnp.exp(steps), extent[axis_at] // blocks).reshape((-1,) + (1,) * (len(extent) - axis_at - 1))

    loudness = one(*shards[0])
    for cut in shards[1:]:
        loudness = loudness * one(*cut)
    return loudness


def bell_draw(stream_key, extent, scale, limit, pieces=(), kind=jnp.bfloat16):
    level = block_levels(stream_key, extent, pieces, -0.22, 0.18) if pieces else 1.0
    values = jax.random.normal(stream_key, extent, jnp.float32) * scale * level
    return jnp.minimum(jnp.maximum(values, -limit), limit).astype(kind)


def setup_inputs(seed: int = 0) -> dict:
    streams_of = jax.random.split(jax.random.key(seed), 13)
    positions = jnp.clip(jax.random.uniform(streams_of[0], (3, SECTORS, BOXES, SLOTS), jnp.float32, -0.9, 0.9) * block_levels(streams_of[0], (3, SECTORS, BOXES, SLOTS), ((1, 4), (2, 8)), -0.4, 0.0), -0.9, 0.9)
    strengths = bell_draw(streams_of[1], (3, SECTORS, BOXES, SLOTS), 1.0, 6.0, ((1, 4), (2, 8)), jnp.float32)
    counts = set_ends(jax.random.randint(streams_of[2], (SECTORS, BOXES), 1, SLOTS + 1), jax.random.fold_in(streams_of[2], 1), 1, SLOTS).astype(jnp.int32)
    cross_slot = draw_cross_slot(jax.random.fold_in(streams_of[12], 71), 0)
    arrive_box = set_ends(jax.random.randint(streams_of[4], (SECTORS, N_BOX * CROSS_DEV), 0, BOX_DEV), jax.random.fold_in(streams_of[4], 1), 0, BOX_DEV - 1).astype(jnp.int32)
    il_source = set_ends(jax.random.randint(streams_of[5], (SECTORS, BOXES, IL), 0, BOX_DEV), jax.random.fold_in(streams_of[5], 1), 0, BOX_DEV - 1).astype(jnp.int32)
    il_class = set_ends(jax.random.randint(streams_of[6], (SECTORS, BOXES, IL), 0, NCLASS), jax.random.fold_in(streams_of[6], 1), 0, NCLASS - 1).astype(jnp.int32)
    m2m = bell_draw(streams_of[7], (4, COEF, COEF), (4 * COEF) ** -0.5, 0.125)
    m2l_leaf = bell_draw(streams_of[8], (NCLASS, COEF, COEF), (16 * COEF) ** -0.5, 0.0625)
    tree_up = bell_draw(streams_of[9], (2, COEF, COEF), (2 * COEF) ** -0.5, 0.21875)
    tree_m2l = bell_draw(streams_of[10], (2, COEF, COEF), COEF ** -0.5, 0.25)
    m2l_sector = bell_draw(streams_of[11], (SECTORS - 1, COEF, COEF), ((SECTORS - 1) * COEF) ** -0.5, 0.15625)
    return {"positions": positions, "strengths": strengths, "counts": counts, "cross_slot": cross_slot, "arrive_box": arrive_box, "il_source": il_source, "il_class": il_class, "m2m": m2m, "m2l_leaf": m2l_leaf, "tree_up": tree_up, "tree_m2l": tree_m2l, "m2l_sector": m2l_sector}


DELTA_SQ = 0.25
TIME_STEP = 0.02
INV_FOUR_PI = 1.0 / (4.0 * math.pi)
HIGHEST_PRECISION = lax.Precision.HIGHEST
OFFSETS = ((0.0, 0.0, 0.0), (0.0, 0.0, -2.0), (0.0, 0.0, 2.0), (-2.0, 0.0, 0.0), (2.0, 0.0, 0.0))

def chebyshev(coordinate):
    scaled = 0.5 * coordinate
    series = [jnp.ones_like(scaled), scaled]
    for order in range(2, TERMS):
        series.append(2.0 * scaled * series[-1] - series[-2])
    return jnp.stack(series[:TERMS])

def multipoles(cheb_a, cheb_b, weights):
    weighted = weights[:, None] * cheb_a[None]
    return jnp.einsum('cjnp,knp->ncjk', weighted, cheb_b, precision=HIGHEST_PRECISION)

def evaluate(local, cheb_a, cheb_b):
    shaped = local.reshape(local.shape[0], 3, TERMS, TERMS)
    partial_sum = jnp.einsum('ncjk,knp->cjnp', shaped, cheb_b, precision=HIGHEST_PRECISION)
    return lax.optimization_barrier(jnp.sum(partial_sum * cheb_a[None], axis=1)) / TERMS

def pair_velocity(target, source, weight, offset):
    delta_x = target[0][:, :, None] - (source[0][:, None, :] + offset[0])
    delta_y = target[1][:, :, None] - (source[1][:, None, :] + offset[1])
    delta_z = target[2][:, :, None] - (source[2][:, None, :] + offset[2])
    radius_sq = delta_x * delta_x + delta_y * delta_y + delta_z * delta_z + DELTA_SQ
    inverse = INV_FOUR_PI / (radius_sq * jnp.sqrt(radius_sq))
    weight_x = weight[0][:, None, :]
    weight_y = weight[1][:, None, :]
    weight_z = weight[2][:, None, :]
    speed_x = lax.optimization_barrier(jnp.sum(inverse * (weight_y * delta_z - weight_z * delta_y), axis=2))
    speed_y = lax.optimization_barrier(jnp.sum(inverse * (weight_z * delta_x - weight_x * delta_z), axis=2))
    speed_z = lax.optimization_barrier(jnp.sum(inverse * (weight_x * delta_y - weight_y * delta_x), axis=2))
    return jnp.stack([speed_x, speed_y, speed_z])

def near_velocity(places, weights):
    sectors, boxes, slots = (places.shape[1], places.shape[2], places.shape[3])
    stacked = jnp.concatenate([places, weights], axis=0)
    zero_box = jnp.zeros_like(stacked[:, :, :1])
    lower = jnp.concatenate([zero_box, stacked[:, :, :-1]], axis=2)
    upper = jnp.concatenate([stacked[:, :, 1:], zero_box], axis=2)
    sources = [stacked, lower, upper, jnp.roll(stacked, 1, axis=1), jnp.roll(stacked, -1, axis=1)]
    total_boxes = sectors * boxes
    block = math.gcd(total_boxes, 64)

    def arrange(array):
        return array.reshape(array.shape[0], total_boxes // block, block, slots).transpose(1, 0, 2, 3)
    inputs = (arrange(places),) + tuple((arrange(item) for item in sources))

    def block_velocity(items):
        summed = jnp.zeros_like(items[0])
        for index in range(5):
            summed = summed + pair_velocity(items[0], items[1 + index][:3], items[1 + index][3:], OFFSETS[index])
        return summed
    result = lax.map(block_velocity, inputs)
    return result.transpose(1, 0, 2, 3).reshape(3, sectors, boxes, slots)

def far_velocity(places, weights, arrival_terms, il_global, il_class, m2m, m2l_leaf, tree_up, tree_m2l, m2l_sector):
    sectors, boxes = (places.shape[1], places.shape[2])
    coef = TERMS * TERMS
    by_sector_places = places.transpose(1, 0, 2, 3)
    by_sector_weights = weights.transpose(1, 0, 2, 3)

    def leaf_side(items):
        place, weight, arrived = items
        cheb_a = chebyshev(place[0])
        cheb_b = chebyshev(place[1])
        return (multipoles(cheb_a, cheb_b, weight) + arrived).reshape(boxes, 3, coef).astype(jnp.bfloat16)
    leaf = lax.map(leaf_side, (by_sector_places, by_sector_weights, arrival_terms))
    m2m_wide = m2m.astype(jnp.float32)
    level = leaf
    for depth in range(LEVELS_DEV):
        grouped = level.reshape(sectors, -1, 4, 3, coef).astype(jnp.float32)
        level = jnp.einsum('sgocx,oxy->sgcy', grouped, m2m_wide).astype(jnp.bfloat16)
    groups = boxes // BOX_DEV
    depth_count = groups.bit_length() - 1
    up_wide = tree_up.astype(jnp.float32)
    tree_levels = [level]
    for depth in range(depth_count):
        paired = tree_levels[-1].reshape(sectors, -1, 2, 3, coef).astype(jnp.float32)
        merged = jnp.einsum('sncx,xy->sncy', paired[:, :, 0], up_wide[0]) + jnp.einsum('sncx,xy->sncy', paired[:, :, 1], up_wide[1])
        tree_levels.append(merged.astype(jnp.bfloat16))
    roots = tree_levels[-1][:, 0].astype(jnp.float32)
    sector_wide = m2l_sector.astype(jnp.float32)
    far_sum = jnp.zeros((sectors, 3, coef), jnp.float32)
    for distance in range(1, sectors):
        far_sum = far_sum + jnp.einsum('scx,xy->scy', jnp.roll(roots, -distance, axis=0), sector_wide[distance - 1])
    local = far_sum.astype(jnp.bfloat16)[:, None]
    cross_wide = tree_m2l.astype(jnp.float32)
    for depth in reversed(range(depth_count)):
        node_level = tree_levels[depth].reshape(sectors, -1, 2, 3, coef).astype(jnp.float32)
        parent = local.astype(jnp.float32)
        first = jnp.einsum('sncy,xy->sncx', parent, up_wide[0]) + jnp.einsum('sncx,xy->sncy', node_level[:, :, 1], cross_wide[0])
        second = jnp.einsum('sncy,xy->sncx', parent, up_wide[1]) + jnp.einsum('sncx,xy->sncy', node_level[:, :, 0], cross_wide[1])
        local = jnp.stack([first, second], axis=2).reshape(sectors, -1, 3, coef).astype(jnp.bfloat16)
    for depth in range(LEVELS_DEV - 1):
        local = jnp.einsum('sgcy,oxy->sgocx', local.astype(jnp.float32), m2m_wide).reshape(sectors, -1, 3, coef).astype(jnp.bfloat16)
    leaf_wide = m2l_leaf.astype(jnp.float32)

    def leaf_down(items):
        parent, leaf_terms, place, sources, classes = items
        child = jnp.einsum('gcy,oxy->gocx', parent.astype(jnp.float32), m2m_wide).reshape(boxes, 3, coef)
        gathered = leaf_terms.reshape(boxes, 3 * coef)[sources].astype(jnp.float32)
        class_hit = (classes[:, :, None] == jnp.arange(NCLASS, dtype=jnp.int32)[None, None, :]).astype(jnp.float32)
        presum = jnp.einsum('bic,bix->cbx', class_hit, gathered).astype(jnp.bfloat16)
        presum = presum.reshape(NCLASS, boxes * 3, coef).astype(jnp.float32)
        translated = jnp.einsum('cnx,cxy->ny', presum, leaf_wide).reshape(boxes, 3, coef)
        cheb_a = chebyshev(place[0])
        cheb_b = chebyshev(place[1])
        return evaluate(child + translated, cheb_a, cheb_b)
    speeds = lax.map(leaf_down, (local, leaf, by_sector_places, il_global, il_class))
    return speeds.transpose(1, 0, 2, 3)

def reference(positions, strengths, counts, cross_slot, arrive_box, il_source, il_class, m2m, m2l_leaf, tree_up, tree_m2l, m2l_sector):
    sectors, boxes, slots = (positions.shape[1], positions.shape[2], positions.shape[3])
    groups = boxes // BOX_DEV
    slot_ids = jnp.arange(slots, dtype=jnp.int32)
    present = (slot_ids[None, None, :] < counts[:, :, None]).astype(jnp.float32)
    crossing = cross_slot.reshape(sectors, groups, CROSS_DEV)
    flat_present = present.reshape(sectors, groups, BOX_DEV * slots)
    sector_ids = jnp.arange(sectors, dtype=jnp.int32)[:, None, None]
    group_ids = jnp.arange(groups, dtype=jnp.int32)[None, :, None]
    departed = jnp.zeros((sectors, groups, BOX_DEV * slots), jnp.float32).at[sector_ids, group_ids, crossing].set(1.0)
    live = (flat_present * (1.0 - departed)).reshape(sectors, boxes, slots)
    flat_places = positions.reshape(3, sectors, groups, BOX_DEV * slots)
    flat_strength = strengths.reshape(3, sectors, groups, BOX_DEV * slots)
    leave_places = jnp.take_along_axis(flat_places, crossing[None], axis=3)
    leave_present = jnp.take_along_axis(flat_present, crossing, axis=2)
    leave_weights = jnp.take_along_axis(flat_strength, crossing[None], axis=3) * leave_present[None]
    arrive_places = jnp.roll(leave_places, 1, axis=1).reshape(3, sectors, groups * CROSS_DEV)
    arrive_weights = jnp.roll(leave_weights, 1, axis=1).reshape(3, sectors, groups * CROSS_DEV)
    arrive_global = (group_ids * BOX_DEV + arrive_box.reshape(sectors, groups, CROSS_DEV)).reshape(sectors, groups * CROSS_DEV)

    def arrival_side(items):
        place, weight, landing = items
        cheb_a = chebyshev(place[0][:, None])
        cheb_b = chebyshev(place[1][:, None])
        each = multipoles(cheb_a, cheb_b, weight[:, :, None])
        return jax.ops.segment_sum(each, landing, num_segments=boxes)
    arrival_terms = lax.map(arrival_side, (arrive_places.transpose(1, 0, 2), arrive_weights.transpose(1, 0, 2), arrive_global))
    box_base = (jnp.arange(boxes, dtype=jnp.int32) // BOX_DEV * BOX_DEV)[None, :, None]
    il_global = box_base + il_source
    weights = strengths * live[None]
    places = positions
    velocity = jnp.zeros_like(positions)
    for substep in range(2):
        near = near_velocity(places, weights)
        far = far_velocity(places, weights, arrival_terms, il_global, il_class, m2m, m2l_leaf, tree_up, tree_m2l, m2l_sector)
        velocity = near + far
        places = places + TIME_STEP * velocity
    return (places, velocity)
```

```python
import functools
import math

import jax
import jax.numpy as jnp
from jax import lax
from jax.experimental import pallas as pl
from jax.experimental.pallas import tpu as pltpu
from jax.sharding import PartitionSpec as P

TERMS = 21
TERMS_PAD = 24
LEVELS_DEV = 3
NCLASS = 4
COMP_PAD = 4

DELTA_SQ = 0.25
TIME_STEP = 0.02
INV_FOUR_PI = 1.0 / (4.0 * math.pi)
OFFSETS = ((0.0, 0.0, 0.0), (0.0, 0.0, -2.0), (0.0, 0.0, 2.0), (-2.0, 0.0, 0.0), (2.0, 0.0, 0.0))
PIECES = 16
F32 = jnp.float32
BF16 = jnp.bfloat16
NN = (((1,), (0,)), ((), ()))
NT = (((1,), (1,)), ((), ()))
TN = (((0,), (0,)), ((), ()))


def rounded(value):
    return value.astype(BF16).astype(F32)


def matmul(left, right, dims=NN):
    return lax.dot_general(left, right, dims, preferred_element_type=F32)


def digit_reversed(value):
    out = value & 3
    for level in range(1, LEVELS_DEV):
        out = out * 4 + (lax.shift_right_logical(value, 2 * level) & 3)
    return out


def iota(shape, dim):
    return lax.broadcasted_iota(jnp.int32, shape, dim)


def coefficient_spread(coef, wide):
    column = iota((1, coef), 1)
    target = column + (TERMS_PAD - TERMS) * lax.shift_right_logical(column * 3121, 16)
    return (iota((wide, coef), 0) == target).astype(F32).astype(BF16)


def chebyshev_series(coordinate):
    scaled = 0.5 * coordinate
    series = [jnp.ones_like(scaled), scaled]
    for _ in range(2, TERMS):
        series.append(2.0 * scaled * series[-1] - series[-2])
    return series


def fill_chebyshev(ref, coordinate):
    boxes = coordinate.shape[0]
    for order, term in enumerate(chebyshev_series(coordinate)):
        ref[order * boxes : (order + 1) * boxes, :] = term
    ref[TERMS * boxes :, :] = jnp.zeros(((TERMS_PAD - TERMS) * boxes, coordinate.shape[1]), F32)


def outer_terms(cheb_a, cheb_b):
    lanes = cheb_a.shape[1]
    product = (cheb_a[:TERMS, None, :] * cheb_b[None, :, :]).reshape(TERMS * TERMS_PAD, lanes)
    fill = -product.shape[0] % 128
    return jnp.concatenate([product, jnp.zeros((fill, lanes), F32)], axis=0).astype(BF16)


def box_terms(cheb_a_ref, cheb_b_ref, box, boxes):
    rows = pl.ds(box, TERMS_PAD, stride=boxes)
    return outer_terms(cheb_a_ref[rows, :], cheb_b_ref[rows, :])


def high_low(value):
    high = rounded(value)
    return jnp.concatenate([high, value - high], axis=0).astype(BF16)


def leaf_rows(cheb_a_ref, cheb_b_ref, spread_weights_ref, leaf_ref, boxes):
    first = iota((8, 1), 0) < COMP_PAD

    def pair(index, carry):
        rows = pl.ds(pl.multiple_of(index * 8, 8), 8)
        weights = high_low(spread_weights_ref[rows, :])
        summed = []
        for half in range(2):
            box = digit_reversed(index * 2 + half)
            both = matmul(weights, box_terms(cheb_a_ref, cheb_b_ref, box, boxes), NT)
            summed.append(both[:8] + both[8:])
        leaf_ref[rows, :] = jnp.where(first, summed[0], summed[1])
        return carry

    lax.fori_loop(0, boxes // 2, pair, 0, unroll=2)


def upward(leaf_rounded, m2m_ref):
    current = leaf_rounded
    for _ in range(LEVELS_DEV):
        count = current.shape[0] // 4
        total = jnp.zeros((count, current.shape[1]), F32)
        for child in range(4):
            total = total + matmul(
                current[child * count : (child + 1) * count].astype(BF16), m2m_ref[child]
            )
        current = rounded(total)
    return current


def prepare_kernel(
    positions_ref, strengths_ref, counts_ref, cross_ref, weights_ref, spread_ref, message_ref, low_ref, high_ref
):
    _, boxes, slots = positions_ref.shape
    entries = cross_ref.shape[1]
    cross = cross_ref[...]
    shift = slots.bit_length() - 1
    box_hit = iota((boxes, entries), 0) == lax.shift_right_logical(cross, shift)
    slot_hit = iota((slots, entries), 0) == (cross & (slots - 1))
    box_one = box_hit.astype(F32).astype(BF16)
    slot_one = slot_hit.astype(F32).astype(BF16)
    departed = matmul(box_one, slot_one, NT)
    square = (boxes, boxes)
    counts = jnp.sum(
        jnp.where(iota(square, 0) == iota(square, 1), counts_ref[...].astype(F32), 0.0), axis=1, keepdims=True
    )
    present = iota((boxes, slots), 1).astype(F32) < counts
    live = present & (departed < 0.5)
    for comp in range(3):
        weight = jnp.where(live, strengths_ref[comp], 0.0)
        weights_ref[comp] = weight
    spread_ref[...] = jnp.zeros_like(spread_ref)
    step = boxes // 4
    for first in range(step):
        slot = int(sum(((first >> (2 * d)) & 3) << (2 * (LEVELS_DEV - 1 - d)) for d in range(LEVELS_DEV)))
        for comp in range(3):
            rows = weights_ref[comp, pl.ds(first, 4, stride=step), :]
            spread_ref[pl.ds(slot * COMP_PAD + comp, 4, stride=COMP_PAD), :] = rows
    counted = jnp.sum(jnp.where(box_hit, counts, 0.0), axis=0, keepdims=True)
    leaves = (cross & (slots - 1)).astype(F32) < counted
    gathered = []
    for comp in range(6):
        value = positions_ref[comp] if comp < 3 else strengths_ref[comp - 3]
        high = rounded(value)
        both = jnp.concatenate([high, value - high], axis=1).astype(BF16)
        at_box = matmul(both, box_one, TN)
        picked = jnp.where(slot_hit, at_box[:slots] + at_box[slots:], 0.0)
        line = jnp.sum(picked, axis=0, keepdims=True)
        gathered.append(line if comp < 3 else jnp.where(leaves, line, 0.0))
    lines = jnp.concatenate(gathered, axis=0)
    high = rounded(lines)
    packed = jnp.concatenate([high, lines - high, jnp.zeros((4, entries), F32)], axis=0).astype(BF16)
    for comp in range(3):
        message_ref[comp * boxes : (comp + 1) * boxes, :] = positions_ref[comp].astype(BF16)
        message_ref[(3 + comp) * boxes : (4 + comp) * boxes, :] = weights_ref[comp].astype(BF16)
    for part in range(entries // slots):
        start = 6 * boxes + part * 16
        message_ref[start : start + 16, :] = packed[:, part * slots : (part + 1) * slots]
    pad = jnp.zeros((10, slots), F32)
    for ref, row in ((low_ref, 0), (high_ref, boxes - 1)):
        lines = [positions_ref[c, row : row + 1, :] for c in range(3)]
        lines += [weights_ref[c, row : row + 1, :] for c in range(3)]
        ref[...] = jnp.concatenate(lines + [pad], axis=0).astype(BF16)


def counts_kernel(source_ref, class_ref, out_ref):
    boxes, entries = source_ref.shape
    rows = boxes * COMP_PAD
    source = digit_reversed(source_ref[...])
    kind = class_ref[...]
    columns = iota((boxes, boxes), 1)
    totals = [jnp.zeros((boxes, boxes), F32) for _ in range(NCLASS)]
    for entry in range(entries):
        hit = source[:, entry : entry + 1] == columns
        for which in range(NCLASS):
            good = hit & (kind[:, entry : entry + 1] == which)
            totals[which] = totals[which] + good.astype(F32)
    left_box = digit_reversed(lax.shift_right_logical(iota((rows, boxes), 0), 2))
    left = (left_box == iota((rows, boxes), 1)).astype(F32).astype(BF16)
    right = (iota((boxes, rows), 0) == lax.shift_right_logical(iota((boxes, rows), 1), 2)).astype(F32).astype(BF16)
    same = (iota((rows, rows), 0) & 3) == (iota((rows, rows), 1) & 3)
    for which in range(NCLASS):
        spread = matmul(matmul(left, totals[which].astype(BF16)).astype(BF16), right)
        out_ref[which * rows : (which + 1) * rows, :] = jnp.where(same, spread, 0.0).astype(BF16)


def leaf_kernel(places_ref, spread_ref, leaf_ref, cheb_a_ref, cheb_b_ref):
    boxes = places_ref.shape[1]
    fill_chebyshev(cheb_a_ref, places_ref[0])
    fill_chebyshev(cheb_b_ref, places_ref[1])
    leaf_rows(cheb_a_ref, cheb_b_ref, spread_ref, leaf_ref, boxes)


def root_outputs(total, m2m_ref, multipole_ref, root_ref):
    spread = coefficient_spread(TERMS * TERMS, total.shape[1])
    leaf = matmul(total.astype(BF16), spread)
    multipole_ref[...] = leaf.astype(BF16)
    root = upward(leaf, m2m_ref)[:3].astype(BF16)
    root_ref[...] = jnp.broadcast_to(root[None], root_ref.shape)


def arrive_kernel(message_ref, arrive_ref, leaf_ref, m2m_ref, arrival_ref, multipole_ref, root_ref, *, start):
    rows, wide = leaf_ref.shape
    entries = arrive_ref.shape[1]
    slots = message_ref.shape[1]
    parts = []
    for part in range(entries // slots):
        parts.append(message_ref[start + part * 16 : start + part * 16 + 16, :].astype(F32))
    packed = jnp.concatenate(parts, axis=1)
    lines = packed[0:6] + packed[6:12]
    tail = [jnp.zeros((TERMS_PAD - TERMS, entries), F32)]
    cheb_a = jnp.concatenate(chebyshev_series(lines[0:1]) + tail, axis=0)
    cheb_b = jnp.concatenate(chebyshev_series(lines[1:2]) + tail, axis=0)
    terms = outer_terms(cheb_a, cheb_b)
    blank = jnp.zeros((1, entries), F32)
    eight = jnp.concatenate([lines[3:6], blank, lines[3:6], blank], axis=0)
    strength = jnp.broadcast_to(eight[None], (rows // 8, 8, entries)).reshape(rows, entries)
    landing = lax.shift_right_logical(iota((rows, entries), 0), 2) == digit_reversed(arrive_ref[...])
    placed = jnp.where(landing, strength, 0.0)
    high = placed.astype(BF16)
    low = (placed - high.astype(F32)).astype(BF16)
    arrival = matmul(high, terms, NT) + matmul(low, terms, NT)
    arrival_ref[...] = arrival
    root_outputs(leaf_ref[...] + arrival, m2m_ref, multipole_ref, root_ref)


def again_kernel(
    places_ref, spread_ref, arrival_ref, m2m_ref, multipole_ref, root_ref, cheb_a_ref, cheb_b_ref, leaf_ref
):
    leaf_kernel(places_ref, spread_ref, leaf_ref, cheb_a_ref, cheb_b_ref)
    root_outputs(leaf_ref[...] + arrival_ref[...], m2m_ref, multipole_ref, root_ref)


def near_kernel(
    places_ref,
    weights_ref,
    left_places_ref,
    right_places_ref,
    left_weights_ref,
    right_weights_ref,
    below_places_ref,
    above_places_ref,
    below_weights_ref,
    above_weights_ref,
    near_ref,
    source_ref,
    weight_ref,
    lines_ref,
    sums_ref,
):
    _, boxes, slots = places_ref.shape
    group = 8
    for comp in range(3):
        shift = [offset[comp] for offset in OFFSETS]
        own = places_ref[comp]
        mass = weights_ref[comp]
        rows = slice(comp * boxes, (comp + 1) * boxes)
        lifted = slice((3 + comp) * boxes, (4 + comp) * boxes)
        source_ref[0, comp] = own
        weight_ref[0, comp] = mass
        below = below_places_ref[...][comp : comp + 1].astype(F32)
        above = above_places_ref[...][comp : comp + 1].astype(F32)
        below_mass = below_weights_ref[...][3 + comp : 4 + comp].astype(F32)
        above_mass = above_weights_ref[...][3 + comp : 4 + comp].astype(F32)
        source_ref[1, comp] = jnp.concatenate([below, own[:-1]], axis=0) + shift[1]
        weight_ref[1, comp] = jnp.concatenate([below_mass, mass[:-1]], axis=0)
        source_ref[2, comp] = jnp.concatenate([own[1:], above], axis=0) + shift[2]
        weight_ref[2, comp] = jnp.concatenate([mass[1:], above_mass], axis=0)
        source_ref[3, comp] = left_places_ref[rows, :].astype(F32) + shift[3]
        weight_ref[3, comp] = left_weights_ref[lifted, :].astype(F32)
        source_ref[4, comp] = right_places_ref[rows, :].astype(F32) + shift[4]
        weight_ref[4, comp] = right_weights_ref[lifted, :].astype(F32)

    one = jnp.ones((group, slots), F32)
    zero = jnp.zeros((group, slots), F32)
    lane_row = iota((PIECES * group, slots), 0) & (group - 1)

    def thirds(value):
        first = rounded(value)
        second = rounded(value - first)
        return [first, second, value - first - second]

    def per_group(index, carry):
        rows = pl.ds(pl.multiple_of(index * group, group), group)
        target = []
        square = zero
        for comp in range(3):
            line = places_ref[comp, rows, :]
            first = rounded(line)
            target += [-2.0 * first, -2.0 * first, -2.0 * (line - first)]
            square = square + line * line
        target = jnp.concatenate(target + [one, one, one] + thirds(square) + [zero], axis=0).astype(BF16)
        columns = []
        for variant in range(5):
            source = []
            square = zero + DELTA_SQ
            place = [source_ref[variant, comp, rows, :] for comp in range(3)]
            mass = [weight_ref[variant, comp, rows, :] for comp in range(3)]
            for comp in range(3):
                first = rounded(place[comp])
                source += [first, place[comp] - first, first]
                square = square + place[comp] * place[comp]
            source = jnp.concatenate(source + thirds(square) + [one, one, one, zero], axis=0)
            columns.append(jnp.transpose(source).astype(BF16))
            moment = [
                mass[1] * place[2] - mass[2] * place[1],
                mass[2] * place[0] - mass[0] * place[2],
                mass[0] * place[1] - mass[1] * place[0],
            ]
            for comp, line in enumerate(mass + moment):
                high = rounded(line)
                lines_ref[variant, pl.ds(comp, group, stride=16), :] = high
                lines_ref[variant, pl.ds(8 + comp, group, stride=16), :] = line - high
        for first in range(0, group, 2):
            blocks = [jnp.where(lane_row == first + side, target, jnp.zeros_like(target)) for side in range(2)]
            grid = jnp.concatenate(blocks, axis=1)
            total = [jnp.zeros((16, slots), F32) for _ in range(2)]
            for variant in range(5):
                inverse = lax.rsqrt(matmul(columns[variant], grid))
                strength = (inverse * inverse * inverse).astype(BF16)
                for side in range(2):
                    mass = lines_ref[variant, (first + side) * 16 : (first + side + 1) * 16, :].astype(BF16)
                    total[side] = total[side] + matmul(mass, strength[:, side * slots : (side + 1) * slots])
            for side in range(2):
                sums_ref[pl.ds(pl.multiple_of((index * group + first + side) * 8, 8), 8), :] = (
                    total[side][:8] + total[side][8:]
                )
        return carry

    for variant in range(5):
        for blank in (6, 7, 14, 15):
            lines_ref[variant, pl.ds(blank, group, stride=16), :] = zero
    lax.fori_loop(0, boxes // group, per_group, 0)
    place = [places_ref[comp] for comp in range(3)]
    drift = [sums_ref[pl.ds(comp, boxes, stride=8), :] for comp in range(3)]
    moment = [sums_ref[pl.ds(3 + comp, boxes, stride=8), :] for comp in range(3)]
    near_ref[0] = INV_FOUR_PI * (drift[1] * place[2] - drift[2] * place[1] - moment[0])
    near_ref[1] = INV_FOUR_PI * (drift[2] * place[0] - drift[0] * place[2] - moment[1])
    near_ref[2] = INV_FOUR_PI * (drift[0] * place[1] - drift[1] * place[0] - moment[2])


def far_kernel(
    roots_ref,
    near_ref,
    places_ref,
    multipole_ref,
    pairs_ref,
    m2m_ref,
    m2l_leaf_ref,
    tree_up_ref,
    tree_m2l_ref,
    m2l_sector_ref,
    velocity_ref,
    moved_ref,
    *rest,
    sectors,
    groups,
):
    *messages, nodes_ref, cheb_a_ref, cheb_b_ref, local_ref, far_ref = rest
    _, boxes, slots = places_ref.shape
    coef = TERMS * TERMS
    depth = groups.bit_length() - 1
    sector = lax.axis_index("sector")
    block = lax.axis_index("box")
    order = [int(format(n, "b").zfill(depth)[::-1], 2) if depth else 0 for n in range(groups)]
    nodes = jnp.concatenate(
        [roots_ref[s * groups + order[n]].astype(F32) for n in range(groups) for s in range(sectors)], axis=0
    )
    base = [0]
    for level in range(depth + 1):
        count = nodes.shape[0] // 3
        for n in range(count):
            nodes_ref[base[level] + n, 0:3, :] = nodes[3 * n : 3 * n + 3]
        base.append(base[level] + count)
        if level < depth:
            half = nodes.shape[0] // 2
            nodes = rounded(
                matmul(nodes[:half].astype(BF16), tree_up_ref[0]) + matmul(nodes[half:].astype(BF16), tree_up_ref[1])
            )
    local = jnp.zeros((3, coef), F32)
    for ahead in range(1, sectors):
        other = lax.rem(sector + ahead, sectors)
        local = local + matmul(nodes_ref[base[depth] + other][:3].astype(BF16), m2l_sector_ref[ahead - 1])
    local = local.astype(BF16)
    for level in reversed(range(depth)):
        node = lax.shift_right_logical(block, level)
        side = node & 1
        node = node ^ 1
        place = node & 1
        for bit in range(1, depth - level):
            place = place * 2 + (lax.shift_right_logical(node, bit) & 1)
        sibling = nodes_ref[base[level] + place * sectors + sector][:3].astype(BF16)
        local = (matmul(local, tree_up_ref[side], NT) + matmul(sibling, tree_m2l_ref[side])).astype(BF16)
    current = jnp.concatenate([local.astype(F32), jnp.zeros((COMP_PAD - 3, coef), F32)], axis=0)
    for level in range(LEVELS_DEV):
        parent = current.astype(BF16)
        current = jnp.concatenate([matmul(parent, m2m_ref[child], NT) for child in range(4)], axis=0)
    rows = boxes * COMP_PAD
    for which in range(NCLASS):
        presum = matmul(pairs_ref[which * rows : (which + 1) * rows, :], multipole_ref[...]).astype(BF16)
        current = current + matmul(presum, m2l_leaf_ref[which])
    wide = local_ref.shape[2]
    spread = coefficient_spread(coef, wide)
    high = rounded(current)
    local_ref[0] = matmul(high.astype(BF16), spread, NT)
    local_ref[1] = matmul((current - high).astype(BF16), spread, NT)
    fill_chebyshev(cheb_a_ref, places_ref[0])
    fill_chebyshev(cheb_b_ref, places_ref[1])

    def pair(index, carry):
        group = pl.ds(pl.multiple_of(index * 8, 8), 8)
        local = jnp.concatenate([local_ref[0, group, :], local_ref[1, group, :]], axis=0).astype(BF16)
        for half in range(2):
            box = digit_reversed(index * 2 + half)
            both = matmul(local, box_terms(cheb_a_ref, cheb_b_ref, box, boxes))
            far_ref[pl.ds(pl.multiple_of(box * 8, 8), 8), :] = both[:8] + both[8:]
        return carry

    lax.fori_loop(0, boxes // 2, pair, 0, unroll=2)
    run = boxes // 4
    speed = []
    for comp in range(3):
        parts = []
        for digit in range(4):
            start = digit * run * 8 + (digit % 2) * COMP_PAD + comp
            parts.append(far_ref[pl.ds(start, run, stride=8), :])
        velocity = near_ref[comp] + jnp.concatenate(parts, axis=0) / TERMS
        velocity_ref[comp] = velocity
        moved = places_ref[comp] + TIME_STEP * velocity
        moved_ref[comp] = moved
        speed.append(moved)
    if messages:
        message_ref, low_ref, high_ref = messages
        for comp in range(3):
            message_ref[comp * boxes : (comp + 1) * boxes, :] = speed[comp].astype(BF16)
        pad = jnp.zeros((13, slots), F32)
        low_ref[...] = jnp.concatenate([m[:1] for m in speed] + [pad], axis=0).astype(BF16)
        high_ref[...] = jnp.concatenate([m[-1:] for m in speed] + [pad], axis=0).astype(BF16)


def halo(message, low, high):
    sectors, groups = lax.axis_size("sector"), lax.axis_size("box")
    up = [(i, (i + 1) % sectors) for i in range(sectors)]
    down = [(j, i) for i, j in up]
    along = [(i, i + 1) for i in range(groups - 1)]
    back = [(j, i) for i, j in along]
    return (
        lax.ppermute(message, "sector", up),
        lax.ppermute(message, "sector", down),
        lax.ppermute(high, "box", along),
        lax.ppermute(low, "box", back),
    )


def per_device(
    positions,
    strengths,
    counts,
    cross_slot,
    arrive_box,
    il_source,
    il_class,
    m2m,
    m2l_leaf,
    tree_up,
    tree_m2l,
    m2l_sector,
):
    sectors, groups = lax.axis_size("sector"), lax.axis_size("box")
    devices = sectors * groups
    _, _, boxes, slots = positions.shape
    entries = cross_slot.shape[1]
    coef = m2m.shape[-1]
    wide = -(-TERMS * TERMS_PAD // 128) * 128
    rows = boxes * COMP_PAD
    field = jax.ShapeDtypeStruct((3, boxes, slots), F32)
    edge = jax.ShapeDtypeStruct((16, slots), BF16)
    leaf_shape = jax.ShapeDtypeStruct((rows, wide), F32)
    multipole_shape = jax.ShapeDtypeStruct((rows, coef), BF16)
    root_shape = jax.ShapeDtypeStruct((devices, 3, coef), BF16)
    cheb = pltpu.VMEM((TERMS_PAD * boxes, slots), F32)

    def call(body, out_shape, scratch=(), name=None, **keys):
        return pl.pallas_call(
            functools.partial(body, **keys) if keys else body,
            out_shape=out_shape,
            scratch_shapes=list(scratch),
            name=name,
        )

    places = positions.reshape(3, boxes, slots)
    weights, spread, message, low, high = call(
        prepare_kernel,
        (
            field,
            jax.ShapeDtypeStruct((rows, slots), F32),
            jax.ShapeDtypeStruct((6 * boxes + entries // slots * 16, slots), BF16),
            edge,
            edge,
        ),
        name="prepare",
    )(places, strengths.reshape(3, boxes, slots), counts, cross_slot)
    left, right, below, above = halo(message, low, high)
    pairs = call(counts_kernel, jax.ShapeDtypeStruct((NCLASS * rows, rows), BF16), name="pair_counts")(
        il_source.reshape(boxes, -1), il_class.reshape(boxes, -1)
    )
    leaf = call(leaf_kernel, leaf_shape, (cheb, cheb), name="leaf")(places, spread)
    arrival, multipole, root = call(
        arrive_kernel, (leaf_shape, multipole_shape, root_shape), name="arrive", start=6 * boxes
    )(left, arrive_box, leaf, m2m)
    halo_weights = (left, right)
    edge_weights = (below, above)
    halo_places = (left, right)
    edge_places = (below, above)
    velocity = None
    for substep in range(2):
        if substep:
            multipole, root = call(
                again_kernel,
                (multipole_shape, root_shape),
                (cheb, cheb, pltpu.VMEM((rows, wide), F32)),
                name="again",
            )(places, spread, arrival, m2m)
        roots = lax.all_to_all(root, ("sector", "box"), 0, 0, tiled=True)
        near = call(
            near_kernel,
            field,
            (
                pltpu.VMEM((5, 3, boxes, slots), F32),
                pltpu.VMEM((5, 3, boxes, slots), F32),
                pltpu.VMEM((5, 8 * 16, slots), F32),
                pltpu.VMEM((boxes * 8, slots), F32),
            ),
            name="near",
        )(places, weights, *halo_places, *halo_weights, *edge_places, *edge_weights)
        extra = ()
        if substep == 0:
            extra = (jax.ShapeDtypeStruct((3 * boxes, slots), BF16), edge, edge)
        velocity, places, *sent = call(
            far_kernel,
            (field, field) + extra,
            (
                pltpu.VMEM((2 * devices, 8, coef), F32),
                cheb,
                cheb,
                pltpu.VMEM((2, rows, wide), F32),
                pltpu.VMEM((boxes * 8, slots), F32),
            ),
            name="far",
            sectors=sectors,
            groups=groups,
        )(roots, near, places, multipole, pairs, m2m, m2l_leaf, tree_up, tree_m2l, m2l_sector)
        if substep == 0:
            left, right, below, above = halo(*sent)
            halo_places = (left, right)
            edge_places = (below, above)
    return (places[:, None], velocity[:, None])


def solution(mesh):
    placed = (
        P(None, "sector", "box", None),
        P(None, "sector", "box", None),
        P("sector", "box"),
        P("sector", "box"),
        P("sector", "box"),
        P("sector", "box", None),
        P("sector", "box", None),
        P(),
        P(),
        P(),
        P(),
        P(),
    )
    return jax.shard_map(
        per_device,
        mesh=mesh,
        in_specs=placed,
        out_specs=(P(None, "sector", "box", None), P(None, "sector", "box", None)),
        check_vma=False,
    )
```
